1024 devices in a mesh: dp: 64 (over z, x_lo, core), fsdp: 16 (over x_hi, y).
Axes of the slice: x: 8 (x_hi: 2, x_lo: 4; x = x_hi * 4 + x_lo), y: 8, z: 8, core: 2. Of those that a mesh axis runs over, the one named last changes fastest.
Arguments:
- patches: bfloat16 [262144, 384], P(('dp', 'fsdp')), may hold values from -24 to 24
- grad_embed: bfloat16 [262144, 3072], P(('dp', 'fsdp')), may hold values from -6 to 6
- weight: bfloat16 [384, 3072], P(None, 'fsdp'), may hold values from -0.3125 to 0.3125
- straggler: int32 [64], P('dp'), may hold values 0 or 1
- decode: int32 [64], P('dp'), may hold values from 1 to 3
- encode: int32 [64, 2], P('dp'), may hold values from 1 to 3
Outputs:
- embedded: bfloat16 [262144, 3072], P(('dp', 'fsdp'))
- weight_grad: float32 [384, 3072], P('dp', 'fsdp')
The draws below stay inside these ranges and needn't reach their ends.
All inputs are finite; a program needn't handle non-finite values. No bound on the sum of `straggler` on one device may be relied on, other than what follows from the above.
Results may differ from the reference program's by a relative error of at most 0.001.
Values may be sent and summed in bfloat16 or wider, within the bound.
A program may use at most 32 MiB of HBM per device.

```python
import jax
import jax.numpy as jnp
from jax import lax

P_SIZE = 384
DW = 3072
REP_TOK = 4096
TOKENS = 262144
N_DP = 64


def place_ends(entries, key, least, top_value):
    longest = entries.shape.index(max(entries.shape))
    spots = []
    for shift in (0, 1):
        where = [jax.random.randint(jax.random.fold_in(key, axis), (), 0, length) for axis, length in enumerate(entries.shape)]
        where[longest] = (where[longest] + shift) % entries.shape[longest]
        spots.append(tuple(where))
    return entries.at[spots[0]].set(least).at[spots[1]].set(top_value)


def raised(array, key, source, target, shards_of, factor):
    def block_of(dim):
        return (jnp.arange(array.shape[dim]) // (array.shape[dim] // shards_of)).reshape((-1,) + (1,) * (array.ndim - 1 - dim))

    one_side = jax.random.permutation(key, shards_of)[block_of(target)]
    other_side = (block_of(target) + shards_of // 2) % shards_of
    return jnp.where((block_of(source) == one_side) | (block_of(source) == other_side), factor * array, array)


def block_scale(stream_key, dims, shards, smallest, top_value):
    loudness, own = 1.0, jax.random.fold_in(stream_key, 6)
    for axis_at, shards_of in shards:
        steps = jnp.exp(jax.random.uniform(jax.random.fold_in(own, axis_at), (shards_of,), jnp.float32, smallest / len(shards), top_value / len(shards)))
        loudness = loudness * jnp.repeat(steps, dims[axis_at] // shards_of).reshape([-1 if axis == axis_at else 1 for axis in range(len(dims))])
    return loudness


def scatter_about(key, extent, spread, bound, shards=(), dtype=jnp.bfloat16):
    level = block_scale(key, extent, shards, -0.22, 0.18) if shards else 1.0
    entries = jax.random.normal(key, extent, jnp.float32) * spread * level
    return jnp.minimum(jnp.maximum(entries, -bound), bound).astype(dtype)


def heavy_noise(key, dims, spread, limit, pieces, heavy, held_as=jnp.bfloat16):
    array = spread * jax.random.normal(key, dims, jnp.float32)
    if pieces:
        array = array * block_scale(key, dims, pieces, -0.22, 0.18)
    return jnp.clip(raised(array, jax.random.fold_in(key, 3), *heavy), -limit, limit).astype(held_as)


def setup_inputs(seed: int = 0) -> dict:
    key_of = jax.random.split(jax.random.key(seed), 7)
    patches = heavy_noise(key_of[0], (TOKENS, P_SIZE), 1.0, 24.0, ((0, 1024),), (0, 1, 128, 5.5))
    grad_embed = scatter_about(key_of[1], (TOKENS, DW), 1.0, 6.0, ((0, 1024),))
    weight = scatter_about(key_of[2], (P_SIZE, DW), P_SIZE ** -0.5, 0.3125, ((1, 16),))
    straggler = place_ends((jax.random.randint(key_of[3], (N_DP,), 0, 8) < 7).astype(jnp.int32), jax.random.fold_in(key_of[3], 1), 0, 1)
    decode = place_ends(jax.random.randint(key_of[4], (N_DP,), 1, 4), jax.random.fold_in(key_of[4], 1), 1, 3).astype(jnp.int32)
    encode = place_ends(jax.random.randint(key_of[5], (N_DP, 2), 1, 4), jax.random.fold_in(key_of[5], 1), 1, 3).astype(jnp.int32)
    return dict(patches=patches, grad_embed=grad_embed, weight=weight, straggler=straggler, decode=decode, encode=encode)


def reference(patches, grad_embed, weight, straggler, decode, encode):
    embedded = jnp.dot(patches, weight, preferred_element_type=jnp.float32).astype(jnp.bfloat16)
    served = straggler * decode
    factor = served * encode[:, 0] + jnp.roll(served * encode[:, 1], 1)
    scales = factor.astype(jnp.float32) / REP_TOK
    inputs = patches.reshape(N_DP, REP_TOK, P_SIZE)
    cotans = grad_embed.reshape(N_DP, REP_TOK, DW)

    def accumulate(total, items):
        inner, outer, scale = items
        term = lax.dot_general(inner, outer, (((0,), (0,)), ((), ())), preferred_element_type=jnp.float32)
        return total + scale * term, None

    start = jnp.zeros((P_SIZE, DW), jnp.float32)
    weight_grad, unused = lax.scan(accumulate, start, (inputs, cotans, scales))
    return embedded, weight_grad
```

```python
import jax
import jax.numpy as jnp
from jax import lax
from jax.experimental import pallas as pl
from jax.experimental.pallas import tpu as pltpu
from jax.sharding import PartitionSpec as P

MESH = pl.DeviceIdType.MESH
F32 = jnp.float32
BF16 = jnp.bfloat16
RING = 8
X_LO = 4
P_SIZE = 384
DW = 3072
TOK = 256
SHARD = DW // 16
HALF = SHARD // 2
COLS = 2 * SHARD
PIECE = 96
PH = PIECE // 2
PLUS, MINUS = 0, 1
STEP = (1, -1)


def hops(first, way):
    return 4 if (first == 0) == (way == PLUS) else 3


def kernel(strag, decode, encode, p_hbm, g_hbm, w_hbm, emb_hbm, out_ref,
           g, p, gsib, psib, wt, t, r1, s, s2, r2, u, s3, r3, emb, ptb, msg, msgs,
           lsem, msem_s, msem_r, tsem_s, tsem_r, xsem_s, xsem_r, asem_s, asem_r, bsem_s, bsem_r,
           sem1_s, sem1_r, sem2_s, sem2_r, sem3_s, sem3_r):
    dp, fs = lax.axis_index("dp"), lax.axis_index("fsdp")
    core = lax.rem(dp, 2)
    xl = lax.rem(lax.div(dp, 2), X_LO)
    z = lax.div(dp, 2 * X_LO)
    xh = lax.div(fs, RING)
    y = lax.rem(fs, RING)
    x = xh * X_LO + xl

    def wrap(v):
        return lax.rem(v + RING, RING)

    def dev(x_, y_, z_, c_):
        return (z_ * 2 * X_LO + lax.rem(x_, X_LO) * 2 + c_, lax.div(x_, X_LO) * RING + y_)

    sib = (dp + 1 - 2 * core, fs)
    chip = lax.div(dp, 2)
    chips = 32
    following = lax.rem(chip + 1, chips)
    preceding = lax.rem(chip + chips - 1, chips)

    def remote(src, dst, ss, rs, to):
        return pltpu.make_async_remote_copy(src_ref=src, dst_ref=dst, send_sem=ss, recv_sem=rs,
                                            device_id=to, device_id_type=MESH)

    shard_rows = pl.ds(pl.multiple_of(fs * SHARD, SHARD), SHARD)
    load_w = pltpu.make_async_copy(w_hbm, wt.at[shard_rows], lsem.at[0])
    load_p = pltpu.make_async_copy(p_hbm, p, lsem.at[1])
    load_g = pltpu.make_async_copy(g_hbm, g, lsem.at[2])
    load_w.start()
    load_p.start()
    load_g.start()

    barrier = pltpu.get_barrier_semaphore()
    partners = [sib]
    for k in range(1, RING):
        partners.append(dev(wrap(x + k - RING), y, z, core))
        partners.append(dev(x, y, wrap(z + k - RING), core))
        partners.append(dev(x, wrap(y + k - RING), z, core))
        partners.append(dev(x, wrap(y + k - RING), z, 1 - core))
    for other in (following, preceding):
        partners.append((2 * other, fs))
        partners.append((2 * other + 1, fs))
    for to in partners:
        pl.semaphore_signal(barrier, inc=1, device_id=to, device_id_type=MESH)

    served = strag[0] * decode[0]
    row = lax.broadcasted_iota(jnp.int32, (8, 128), 0)
    msg[...] = jnp.where(row == 0, served * encode[0, 0], served * encode[0, 1])

    pl.semaphore_wait(barrier, len(partners))

    share_sib = remote(msg, msgs.at[0], msem_s.at[0], msem_r.at[0], sib)
    share_sib.start()
    share_next = [remote(msg, msgs.at[1], msem_s.at[1 + c], msem_r.at[1], (2 * following + c, fs)) for c in (0, 1)]

    @pl.when(core == 1)
    def _():
        for copy in share_next:
            copy.start()

    def unit(x_hi, y_, c_):
        return wt.at[pl.ds(pl.multiple_of((x_hi * RING + y_) * SHARD + c_ * HALF, 32), HALF)]

    xh_of = (xh, 1 - xh)

    def gather_send(kind, way, hop):
        block = unit(xh_of[kind], wrap(y - STEP[way] * hop), core)
        to = dev(x, wrap(y + STEP[way]), z, core)
        return remote(block, block, asem_s.at[kind, way, hop], asem_r.at[kind, way, hop], to)

    def gather_wait(kind, way, hop):
        block = unit(xh_of[kind], wrap(y - STEP[way] * hop), core)
        remote(block, block, asem_s.at[kind, way, hop - 1], asem_r.at[kind, way, hop - 1], sib).wait_recv()

    def pass_on(kind, way, hop, c_):
        block = unit(xh_of[kind], wrap(y - STEP[way] * hop), c_)
        return remote(block, block, bsem_s.at[kind, way, hop], bsem_r.at[kind, way, hop], sib)

    load_w.wait()
    edge = (xl == 0) | (xl == X_LO - 1)
    outward = jnp.where(xl == 0, RING - 1, 1)
    own_unit = unit(xh, y, core)
    cross = [remote(own_unit, own_unit, xsem_s.at[k], xsem_r.at[0],
                    dev(lax.rem(x + (k + 1) * outward, RING), y, z, core)) for k in (0, 1)]

    @pl.when(edge)
    def _():
        for copy in cross:
            copy.start()

    for way in (PLUS, MINUS):
        gather_send(0, way, 0).start()

    load_g.wait()
    load_p.wait()
    tokens = [remote(p, psib, tsem_s.at[2], tsem_r.at[2], sib)]
    for h in (0, 1):
        theirs = pl.ds(pl.multiple_of(h * (DW // 2) + (1 - core) * 2 * COLS, COLS), 2 * COLS)
        tokens.append(remote(g.at[:, theirs], gsib.at[h], tsem_s.at[h], tsem_r.at[h], sib))
    for copy in tokens:
        copy.start()

    feature = lax.broadcasted_iota(jnp.int32, (P_SIZE, P_SIZE), 1)
    twelfth = jnp.right_shift(feature * 43691, 19)
    z_of = jnp.right_shift(feature * 10923, 19)
    place = (twelfth - X_LO * z_of) * PIECE + z_of * 12 + (feature - 12 * twelfth)
    out_row = lax.broadcasted_iota(jnp.int32, (P_SIZE, P_SIZE), 0)
    turn = (
        (out_row == feature).astype(F32).astype(BF16),
        (out_row == place).astype(F32).astype(BF16),
    )

    def features_first(q, tok):
        return lax.dot_general(turn[q], tok, (((1,), (1,)), ((), ())), preferred_element_type=F32).astype(BF16)

    mine = [features_first(q, p[...]) for q in (0, 1)]
    for q in (0, 1):
        ptb[q] = mine[q]

    share_sib.wait_recv()
    remote(msg, msgs.at[1], msem_s.at[1], msem_r.at[1], sib).wait_recv()
    before = msgs[1, 1:2, 0:1]
    first_own, second_own = msg[0:1, 0:1], msg[1:2, 0:1]
    first_sib, second_sib = msgs[0, 0:1, 0:1], msgs[0, 1:2, 0:1]
    lower = core == 0
    scale_own = (first_own + jnp.where(lower, before, second_sib)).astype(F32) / (TOK * 16)
    scale_sib = (first_sib + jnp.where(lower, second_own, before)).astype(F32) / (TOK * 16)

    for copy in tokens:
        copy.wait_recv()
    theirs_t = [features_first(q, psib[...]) for q in (0, 1)]

    pos = (z, x)

    def beside(q, v):
        return dev(x, y, v, core) if q == 0 else dev(v, y, z, core)

    def along(q, h, way, hop):
        n = hops(h, way)
        piece = wrap(pos[q] + STEP[way] * (n - hop))
        src = t.at[q, piece, pl.ds(h * PH, PH)] if hop == 0 else r1.at[q, h, way, hop - 1]
        return piece, remote(src, r1.at[q, h, way, hop], sem1_s.at[q, h, way, hop], sem1_r.at[q, h, way, hop],
                             beside(q, wrap(pos[q] + STEP[way])))

    def along_wait(q, h, way, hop):
        slot = r1.at[q, h, way, hop]
        remote(slot, slot, sem1_s.at[q, h, way, hop], sem1_r.at[q, h, way, hop], sib).wait_recv()

    for q in (0, 1):
        for h in (0, 1):
            here = pl.ds(pl.multiple_of(h * (DW // 2) + core * 2 * COLS + q * COLS, COLS), COLS)
            term = scale_own * jnp.dot(ptb[q], g[:, here], preferred_element_type=F32)
            term += scale_sib * jnp.dot(theirs_t[q], gsib[h, :, q * COLS:(q + 1) * COLS], preferred_element_type=F32)
            if q == 0:
                for k in range(RING):
                    t[0, k, h * PH:(h + 1) * PH, :] = term[k * PH:(k + 1) * PH]
                for way in (PLUS, MINUS):
                    along(0, h, way, 0)[1].start()
            else:
                for k in range(X_LO):
                    t[1, h * X_LO + k, :, :] = term[k * PIECE:(k + 1) * PIECE]
    for h in (0, 1):
        for way in (PLUS, MINUS):
            along(1, h, way, 0)[1].start()

    other_unit = unit(1 - xh, y, core)
    remote(other_unit, other_unit, xsem_s.at[0], xsem_r.at[0], sib).wait_recv()
    for way in (MINUS, PLUS):
        gather_send(1, way, 0).start()
    pass_on(1, PLUS, 0, core).start()

    for hop in range(1, 5):
        for h in (0, 1):
            for way in (PLUS, MINUS):
                for q in (0, 1):
                    n = hops(h, way)
                    if hop < n:
                        along_wait(q, h, way, hop - 1)
                        piece, copy = along(q, h, way, hop)
                        slot = r1.at[q, h, way, hop - 1]
                        slot[...] += t[q, piece, h * PH:(h + 1) * PH, :]
                        copy.start()
                if hop <= hops(h, way):
                    gather_wait(h, way, hop)
                    if hop < hops(h, way):
                        gather_send(h, way, hop).start()
                    pass_on(h, way, hop, core).start()

    pos2 = (x, z)

    def across(q, j):
        k = wrap(pos2[q] + j - RING)
        return remote(s2.at[q, k], r2.at[q, j], sem2_s.at[q, j], sem2_r.at[q, j], beside(1 - q, k))

    for q in (0, 1):
        for h in (0, 1):
            for way in (PLUS, MINUS):
                along_wait(q, h, way, hops(h, way) - 1)
            s[q, h * PH:(h + 1) * PH, :] = (
                t[q, pos[q], h * PH:(h + 1) * PH, :]
                + r1[q, h, PLUS, hops(h, PLUS) - 1] + r1[q, h, MINUS, hops(h, MINUS) - 1]
            )
        s[q, PIECE:PIECE + 8, :] = jnp.zeros((8, COLS), F32)
        for k in range(RING):
            s2[q, k] = s[q, 12 * k:12 * k + 16, :]
        for j in range(1, RING):
            across(q, j).start()

    for kind in (0, 1):
        for way in (PLUS, MINUS):
            for hop in range(1, hops(kind, way) + 1):
                pass_on(kind, way, hop, 1 - core).wait_recv()
    pass_on(1, PLUS, 0, 1 - core).wait_recv()

    def embed(j, carry):
        at = pl.multiple_of(j * COLS, COLS)
        e = lax.dot_general(p[...], wt[pl.ds(at, COLS), :], (((1,), (1,)), ((), ())), preferred_element_type=F32)
        emb[:, pl.ds(at, COLS)] = e.astype(BF16)
        return carry

    lax.fori_loop(0, DW // COLS, embed, 0)
    store = pltpu.make_async_copy(emb, emb_hbm, lsem.at[3])
    store.start()

    def onward(q, par, c_):
        y_to = 4 * core + 2 * q + par
        return y_to, remote(s3.at[q, par, c_], r3.at[y], sem3_s.at[q, par, c_], sem3_r.at[y], dev(x, y_to, z, c_))

    for q in (0, 1):
        for j in range(1, RING):
            across(q, j).wait_recv()
        total = s2[q, pos2[q]]
        for j in range(1, RING):
            total += r2[q, j]
        u[q] = total
        for par in (0, 1):
            for c_ in (0, 1):
                s3[q, par, c_] = u[q, 6 * c_:6 * c_ + 8, par * SHARD:(par + 1) * SHARD]
                y_to, copy = onward(q, par, c_)
                self_ = (y_to == y) & (core == c_)

                @pl.when(self_)
                def _():
                    r3[y] = s3[q, par, c_]

                @pl.when(jnp.logical_not(self_))
                def _():
                    copy.start()

    summed_by = lax.div(y, 4)
    for k in range(RING):
        slot = r3.at[k]

        @pl.when(jnp.logical_not((y == k) & (core == summed_by)))
        def _():
            remote(slot, slot, sem3_s.at[0, 0, 0], sem3_r.at[k], sib).wait_recv()

    total = r3[0]
    for k in range(1, RING):
        total += r3[k]
    out_ref[...] = total[0:6]

    share_sib.wait_send()

    @pl.when(core == 1)
    def _():
        for copy in share_next:
            copy.wait_send()

    @pl.when(edge)
    def _():
        for copy in cross:
            copy.wait_send()

    for copy in tokens:
        copy.wait_send()
    pass_on(1, PLUS, 0, core).wait_send()
    for h in (0, 1):
        for way in (PLUS, MINUS):
            for hop in range(hops(h, way)):
                gather_send(h, way, hop).wait_send()
                pass_on(h, way, hop + 1, core).wait_send()
                for q in (0, 1):
                    along(q, h, way, hop)[1].wait_send()
    for q in (0, 1):
        for j in range(1, RING):
            across(q, j).wait_send()
        for par in (0, 1):
            for c_ in (0, 1):
                y_to, copy = onward(q, par, c_)

                @pl.when(jnp.logical_not((y_to == y) & (core == c_)))
                def _():
                    copy.wait_send()
    store.wait()


def body(patches, grad_embed, weight, straggler, decode, encode):
    any_ = pl.BlockSpec(memory_space=pl.ANY)
    smem = pl.BlockSpec(memory_space=pltpu.SMEM)
    dma = pltpu.SemaphoreType.DMA
    return pl.pallas_call(
        kernel,
        out_shape=(
            jax.ShapeDtypeStruct((TOK, DW), BF16),
            jax.ShapeDtypeStruct((6, SHARD), F32),
        ),
        in_specs=[smem, smem, smem, any_, any_, any_],
        out_specs=(any_, pl.BlockSpec(memory_space=pltpu.VMEM)),
        scratch_shapes=[
            pltpu.VMEM((TOK, DW), BF16),
            pltpu.VMEM((TOK, P_SIZE), BF16),
            pltpu.VMEM((2, TOK, 2 * COLS), BF16),
            pltpu.VMEM((TOK, P_SIZE), BF16),
            pltpu.VMEM((DW, P_SIZE), BF16),
            pltpu.VMEM((2, RING, PIECE, COLS), F32),
            pltpu.VMEM((2, 2, 2, 4, PH, COLS), F32),
            pltpu.VMEM((2, PIECE + 8, COLS), F32),
            pltpu.VMEM((2, RING, 16, COLS), F32),
            pltpu.VMEM((2, RING, 16, COLS), F32),
            pltpu.VMEM((2, 16, COLS), F32),
            pltpu.VMEM((2, 2, 2, 8, SHARD), F32),
            pltpu.VMEM((RING, 8, SHARD), F32),
            pltpu.VMEM((TOK, DW), BF16),
            pltpu.VMEM((2, P_SIZE, TOK), BF16),
            pltpu.VMEM((8, 128), jnp.int32),
            pltpu.VMEM((2, 8, 128), jnp.int32),
            dma((4,)),
            dma((3,)), dma((2,)),
            dma((3,)), dma((3,)),
            dma((2,)), dma((1,)),
            dma((2, 2, 4)), dma((2, 2, 4)),
            dma((2, 2, 5)), dma((2, 2, 5)),
            dma((2, 2, 2, 4)), dma((2, 2, 2, 4)),
            dma((2, RING)), dma((2, RING)),
            dma((2, 2, 2)), dma((RING,)),
        ],
        compiler_params=pltpu.CompilerParams(
            collective_id=0, has_side_effects=True, vmem_limit_bytes=48 * 1024 * 1024
        ),
    )(straggler, decode, encode, patches, grad_embed, weight.T)


def solution(mesh):
    return jax.shard_map(
        body,
        mesh=mesh,
        in_specs=(
            P(("dp", "fsdp"), None),
            P(("dp", "fsdp"), None),
            P(None, "fsdp"),
            P("dp"),
            P("dp"),
            P("dp", None),
        ),
        out_specs=(P(("dp", "fsdp"), None), P("dp", "fsdp")),
        check_vma=False,
    )
```

```python
import jax
import jax.numpy as jnp
from jax import lax
from jax.experimental import pallas as pl
from jax.experimental.pallas import tpu as pltpu
from jax.sharding import PartitionSpec as P

MESH = pl.DeviceIdType.MESH
F32 = jnp.float32
BF16 = jnp.bfloat16
RING = 8
X_LO = 4
P_SIZE = 384
DW = 3072
TOK = 256
SHARD = DW // 16
HALF = SHARD // 2
COLS = 2 * SHARD
PIECE = 96
PH = PIECE // 2
PLUS, MINUS = 0, 1
STEP = (1, -1)
SCALE = 8
I16 = jnp.int16


def hops(first, way):
    return 4 if (first == 0) == (way == PLUS) else 3


def scales(top):
    return jnp.floor(jnp.log2(jnp.maximum(top, 2.0 ** -100))) - 14.0


def code(v):
    e = scales(jnp.max(jnp.abs(v), axis=0, keepdims=True))
    return jnp.clip(jnp.round(v * jnp.exp2(-e)), -32767.0, 32767.0), e


def decoded(ref, rows):
    scale = jnp.exp2(ref[rows:rows + 1, :].astype(jnp.int32).astype(F32))
    return ref[0:rows, :].astype(jnp.int32).astype(F32) * scale


def kernel(strag, decode, enc_hbm, p_hbm, g_hbm, w_hbm, emb, out_ref,
           encode, g, p, gsib, psib, wt, t, q1, r1, s, s2, r2, u, s3, r3, msg, msgs,
           lsem, msem_s, msem_r, tsem_s, tsem_r, xsem_s, xsem_r, asem_s, asem_r, bsem_s, bsem_r,
           sem1_s, sem1_r, sem2_s, sem2_r, sem3_s, sem3_r):
    dp, fs = lax.axis_index("dp"), lax.axis_index("fsdp")
    core = lax.rem(dp, 2)
    xl = lax.rem(lax.div(dp, 2), X_LO)
    z = lax.div(dp, 2 * X_LO)
    xh = lax.div(fs, RING)
    y = lax.rem(fs, RING)
    x = xh * X_LO + xl

    def wrap(v):
        return lax.rem(v + RING, RING)

    def dev(x_, y_, z_, c_):
        return (z_ * 2 * X_LO + lax.rem(x_, X_LO) * 2 + c_, lax.div(x_, X_LO) * RING + y_)

    sib = (dp + 1 - 2 * core, fs)
    chip = lax.div(dp, 2)
    chips = 32
    following = lax.rem(chip + 1, chips)
    preceding = lax.rem(chip + chips - 1, chips)

    def remote(src, dst, ss, rs, to):
        return pltpu.make_async_remote_copy(src_ref=src, dst_ref=dst, send_sem=ss, recv_sem=rs,
                                            device_id=to, device_id_type=MESH)

    shard_rows = pl.ds(pl.multiple_of(fs * SHARD, SHARD), SHARD)
    load_w = pltpu.make_async_copy(w_hbm, wt.at[shard_rows], lsem.at[0])
    load_p = pltpu.make_async_copy(p_hbm, p, lsem.at[1])
    load_g = pltpu.make_async_copy(g_hbm, g, lsem.at[2])
    load_e = pltpu.make_async_copy(enc_hbm, encode, lsem.at[3])
    load_e.start()
    load_w.start()
    load_p.start()
    load_g.start()

    barrier = pltpu.get_barrier_semaphore()
    partners = [sib]
    for k in (1, RING - 1):
        partners.append(dev(wrap(x + k - RING), y, z, core))
        partners.append(dev(x, y, wrap(z + k - RING), core))
        partners.append(dev(x, wrap(y + k - RING), z, core))
        partners.append(dev(lax.rem(x + 2 * k, RING), y, z, core))
    for other in (following, preceding):
        partners.append((2 * other, fs))
        partners.append((2 * other + 1, fs))
    for to in partners:
        pl.semaphore_signal(barrier, inc=1, device_id=to, device_id_type=MESH)

    load_e.wait()
    served = strag[0] * decode[0]
    row = lax.broadcasted_iota(jnp.int32, (8, 128), 0)
    msg[...] = jnp.where(row == 0, served * encode[0, 0], served * encode[0, 1])

    pl.semaphore_wait(barrier, len(partners))

    share_sib = remote(msg, msgs.at[0], msem_s.at[0], msem_r.at[0], sib)
    share_sib.start()
    share_next = [remote(msg, msgs.at[1], msem_s.at[1 + c], msem_r.at[1], (2 * following + c, fs)) for c in (0, 1)]

    @pl.when(core == 1)
    def _():
        for copy in share_next:
            copy.start()

    def unit(x_hi, y_, c_):
        return wt.at[pl.ds(pl.multiple_of((x_hi * RING + y_) * SHARD + c_ * HALF, 32), HALF)]

    xh_of = (xh, 1 - xh)

    def gather_send(kind, way, hop):
        block = unit(xh_of[kind], wrap(y - STEP[way] * hop), core)
        to = dev(x, wrap(y + STEP[way]), z, core)
        return remote(block, block, asem_s.at[kind, way, hop], asem_r.at[kind, way, hop], to)

    def gather_wait(kind, way, hop):
        block = unit(xh_of[kind], wrap(y - STEP[way] * hop), core)
        remote(block, block, asem_s.at[kind, way, hop - 1], asem_r.at[kind, way, hop - 1], sib).wait_recv()

    def pass_on(kind, way, hop, c_):
        block = unit(xh_of[kind], wrap(y - STEP[way] * hop), c_)
        return remote(block, block, bsem_s.at[kind, way, hop], bsem_r.at[kind, way, hop], sib)

    load_w.wait()
    edge = (xl == 0) | (xl == X_LO - 1)
    outward = jnp.where(xl == 0, RING - 1, 1)
    own_unit = unit(xh, y, core)
    cross = [remote(own_unit, own_unit, xsem_s.at[k], xsem_r.at[0],
                    dev(lax.rem(x + (k + 1) * outward, RING), y, z, core)) for k in (0, 1)]

    @pl.when(edge)
    def _():
        for copy in cross:
            copy.start()

    for way in (PLUS, MINUS):
        gather_send(0, way, 0).start()

    load_g.wait()
    load_p.wait()
    tokens = [remote(p, psib, tsem_s.at[2], tsem_r.at[2], sib)]
    for h in (0, 1):
        theirs = pl.ds(pl.multiple_of(h * (DW // 2) + (1 - core) * 2 * COLS, COLS), 2 * COLS)
        tokens.append(remote(g.at[:, theirs], gsib.at[h], tsem_s.at[h], tsem_r.at[h], sib))
    for copy in tokens:
        copy.start()

    feature = lax.broadcasted_iota(jnp.int32, (P_SIZE, P_SIZE), 1)
    twelfth = jnp.right_shift(feature * 43691, 19)
    z_of = jnp.right_shift(feature * 10923, 19)
    place = (twelfth - X_LO * z_of) * PIECE + z_of * 12 + (feature - 12 * twelfth)
    out_row = lax.broadcasted_iota(jnp.int32, (P_SIZE, P_SIZE), 0)
    turn = (
        (out_row == feature).astype(F32).astype(BF16),
        (out_row == place).astype(F32).astype(BF16),
    )

    def features_first(q, tok):
        return lax.dot_general(turn[q], tok, (((1,), (1,)), ((), ())), preferred_element_type=F32).astype(BF16)

    def columns(q, h):
        return pl.ds(pl.multiple_of(h * (DW // 2) + core * 2 * COLS + q * COLS, COLS), COLS)

    for q in (0, 1):
        mine = features_first(q, p[...])
        for h in (0, 1):
            term = jnp.dot(mine, g[:, columns(q, h)], preferred_element_type=F32)
            if q == 0:
                for k in range(RING):
                    t[0, k, h * PH:(h + 1) * PH, :] = term[k * PH:(k + 1) * PH]
            else:
                for k in range(X_LO):
                    t[1, h * X_LO + k, :, :] = term[k * PIECE:(k + 1) * PIECE]

    def gather_hop(kind, hop):
        for way in (PLUS, MINUS):
            if hop <= hops(kind, way):
                gather_wait(kind, way, hop)
                if hop < hops(kind, way):
                    gather_send(kind, way, hop).start()
                pass_on(kind, way, hop, core).start()

    gather_hop(0, 1)

    share_sib.wait_recv()
    remote(msg, msgs.at[1], msem_s.at[1], msem_r.at[1], sib).wait_recv()
    before = msgs[1, 1:2, 0:1]
    first_own, second_own = msg[0:1, 0:1], msg[1:2, 0:1]
    first_sib, second_sib = msgs[0, 0:1, 0:1], msgs[0, 1:2, 0:1]
    lower = core == 0
    scale_own = (first_own + jnp.where(lower, before, second_sib)).astype(F32) / (TOK * 16)
    scale_sib = (first_sib + jnp.where(lower, second_own, before)).astype(F32) / (TOK * 16)

    for copy in tokens:
        copy.wait_recv()

    pos = (z, x)

    def beside(q, v):
        return dev(x, y, v, core) if q == 0 else dev(v, y, z, core)

    def along(q, h, way, hop):
        slot = q1.at[q, h, way, hop]
        return remote(slot, r1.at[q, h, way, hop], sem1_s.at[q, h, way, hop], sem1_r.at[q, h, way, hop],
                      beside(q, wrap(pos[q] + STEP[way])))

    def along_send(q, h, way, hop):
        piece = wrap(pos[q] + STEP[way] * (hops(h, way) - hop))
        v = t[q, piece, h * PH:(h + 1) * PH, :]
        if hop:
            v += decoded(r1.at[q, h, way, hop - 1], PH)
        v, e = code(v)
        q1[q, h, way, hop, 0:PH, :] = v.astype(jnp.int32).astype(I16)
        q1[q, h, way, hop, PH:PH + SCALE, :] = jnp.broadcast_to(e, (SCALE, COLS)).astype(jnp.int32).astype(I16)
        along(q, h, way, hop).start()

    def along_wait(q, h, way, hop):
        slot = r1.at[q, h, way, hop]
        remote(slot, slot, sem1_s.at[q, h, way, hop], sem1_r.at[q, h, way, hop], sib).wait_recv()

    for q in (0, 1):
        others = features_first(q, psib[...])
        for h in (0, 1):
            term = scale_sib * jnp.dot(others, gsib[h, :, q * COLS:(q + 1) * COLS], preferred_element_type=F32)
            if q == 0:
                for k in range(RING):
                    rows = slice(h * PH, (h + 1) * PH)
                    t[0, k, rows, :] = scale_own * t[0, k, rows, :] + term[k * PH:(k + 1) * PH]
                for way in (PLUS, MINUS):
                    along_send(0, h, way, 0)
            else:
                for k in range(X_LO):
                    at = h * X_LO + k
                    t[1, at, :, :] = scale_own * t[1, at, :, :] + term[k * PIECE:(k + 1) * PIECE]
    for h in (0, 1):
        for way in (PLUS, MINUS):
            along_send(1, h, way, 0)

    other_unit = unit(1 - xh, y, core)
    remote(other_unit, other_unit, xsem_s.at[0], xsem_r.at[0], sib).wait_recv()
    for way in (MINUS, PLUS):
        gather_send(1, way, 0).start()
    pass_on(1, PLUS, 0, core).start()

    for hop in range(1, 4):
        for h in (0, 1):
            for way in (PLUS, MINUS):
                for q in (0, 1):
                    if hop < hops(h, way):
                        along_wait(q, h, way, hop - 1)
                        along_send(q, h, way, hop)
        gather_hop(0, hop + 1)
        gather_hop(1, hop)

    pos2 = (x, z)

    def across(q, j):
        k = wrap(pos2[q] + j - RING)
        return remote(s2.at[q, k], r2.at[q, j], sem2_s.at[q, j], sem2_r.at[q, j], beside(1 - q, k))

    for q in (0, 1):
        for h in (0, 1):
            for way in (PLUS, MINUS):
                along_wait(q, h, way, hops(h, way) - 1)
            s[q, h * PH:(h + 1) * PH, :] = (
                t[q, pos[q], h * PH:(h + 1) * PH, :]
                + decoded(r1.at[q, h, PLUS, hops(h, PLUS) - 1], PH) + decoded(r1.at[q, h, MINUS, hops(h, MINUS) - 1], PH)
            )
        s[q, PIECE:PIECE + 8, :] = jnp.zeros((8, COLS), F32)
    data_row = lax.broadcasted_iota(jnp.int32, (16, COLS), 0) < 12
    for q in (0, 1):
        for k in range(RING):
            v = jnp.where(data_row, s[q, 12 * k:12 * k + 16, :], 0.0)
            v, e = code(v)
            s2[q, k] = jnp.where(data_row, v, e).astype(jnp.int32).astype(I16)
        for j in range(1, RING):
            across(q, j).start()
    gather_hop(1, 4)

    for kind in (0, 1):
        for way in (PLUS, MINUS):
            for hop in range(1, hops(kind, way) + 1):
                pass_on(kind, way, hop, 1 - core).wait_recv()
    pass_on(1, PLUS, 0, 1 - core).wait_recv()

    def embed(j, carry):
        at = pl.multiple_of(j * COLS, COLS)
        e = lax.dot_general(p[...], wt[pl.ds(at, COLS), :], (((1,), (1,)), ((), ())), preferred_element_type=F32)
        emb[:, pl.ds(at, COLS)] = e.astype(BF16)
        return carry

    lax.fori_loop(0, DW // COLS, embed, 0)

    def onward(q, par, c_):
        y_to = 4 * core + 2 * q + par
        return y_to, remote(s3.at[q, par, c_], r3.at[y], sem3_s.at[q, par, c_], sem3_r.at[y], dev(x, y_to, z, c_))

    for q in (0, 1):
        for j in range(1, RING):
            across(q, j).wait_recv()
        total = decoded(s2.at[q, pos2[q]], 12)
        for j in range(1, RING):
            total += decoded(r2.at[q, j], 12)
        u[q, 0:12, :] = total
        u[q, 12:16, :] = jnp.zeros((4, COLS), F32)
        for par in (0, 1):
            for c_ in (0, 1):
                s3[q, par, c_] = u[q, 6 * c_:6 * c_ + 8, par * SHARD:(par + 1) * SHARD]
                y_to, copy = onward(q, par, c_)
                self_ = (y_to == y) & (core == c_)

                @pl.when(self_)
                def _():
                    r3[y] = s3[q, par, c_]

                @pl.when(jnp.logical_not(self_))
                def _():
                    copy.start()

    summed_by = lax.div(y, 4)
    for k in range(RING):
        slot = r3.at[k]

        @pl.when(jnp.logical_not((y == k) & (core == summed_by)))
        def _():
            remote(slot, slot, sem3_s.at[0, 0, 0], sem3_r.at[k], sib).wait_recv()

    total = r3[0]
    for k in range(1, RING):
        total += r3[k]
    out_ref[...] = total[0:6]

    share_sib.wait_send()

    @pl.when(core == 1)
    def _():
        for copy in share_next:
            copy.wait_send()

    @pl.when(edge)
    def _():
        for copy in cross:
            copy.wait_send()

    for copy in tokens:
        copy.wait_send()
    pass_on(1, PLUS, 0, core).wait_send()
    for h in (0, 1):
        for way in (PLUS, MINUS):
            for hop in range(hops(h, way)):
                gather_send(h, way, hop).wait_send()
                pass_on(h, way, hop + 1, core).wait_send()
                for q in (0, 1):
                    along(q, h, way, hop).wait_send()
    for q in (0, 1):
        for j in range(1, RING):
            across(q, j).wait_send()
        for par in (0, 1):
            for c_ in (0, 1):
                y_to, copy = onward(q, par, c_)

                @pl.when(jnp.logical_not((y_to == y) & (core == c_)))
                def _():
                    copy.wait_send()


def body(patches, grad_embed, weight, straggler, decode, encode):
    hbm = pl.BlockSpec(memory_space=pltpu.HBM)
    vmem = pl.BlockSpec(memory_space=pltpu.VMEM)
    smem = pl.BlockSpec(memory_space=pltpu.SMEM)
    dma = pltpu.SemaphoreType.DMA
    return pl.pallas_call(
        kernel,
        out_shape=(
            pltpu.VMEM((TOK, DW), BF16),
            pltpu.VMEM((6, SHARD), F32),
        ),
        in_specs=[smem, smem, hbm, hbm, hbm, hbm],
        out_specs=(vmem, vmem),
        scratch_shapes=[
            pltpu.SMEM((1, 2), jnp.int32),
            pltpu.VMEM((TOK, DW), BF16),
            pltpu.VMEM((TOK, P_SIZE), BF16),
            pltpu.VMEM((2, TOK, 2 * COLS), BF16),
            pltpu.VMEM((TOK, P_SIZE), BF16),
            pltpu.VMEM((DW, P_SIZE), BF16),
            pltpu.VMEM((2, RING, PIECE, COLS), F32),
            pltpu.VMEM((2, 2, 2, 4, PH + SCALE, COLS), I16),
            pltpu.VMEM((2, 2, 2, 4, PH + SCALE, COLS), I16),
            pltpu.VMEM((2, PIECE + 8, COLS), F32),
            pltpu.VMEM((2, RING, 16, COLS), I16),
            pltpu.VMEM((2, RING, 16, COLS), I16),
            pltpu.VMEM((2, 16, COLS), F32),
            pltpu.VMEM((2, 2, 2, 8, SHARD), F32),
            pltpu.VMEM((RING, 8, SHARD), F32),
            pltpu.VMEM((8, 128), jnp.int32),
            pltpu.VMEM((2, 8, 128), jnp.int32),
            dma((4,)),
            dma((3,)), dma((2,)),
            dma((3,)), dma((3,)),
            dma((2,)), dma((1,)),
            dma((2, 2, 4)), dma((2, 2, 4)),
            dma((2, 2, 5)), dma((2, 2, 5)),
            dma((2, 2, 2, 4)), dma((2, 2, 2, 4)),
            dma((2, RING)), dma((2, RING)),
            dma((2, 2, 2)), dma((RING,)),
        ],
        compiler_params=pltpu.CompilerParams(
            collective_id=0, has_side_effects=True, vmem_limit_bytes=48 * 1024 * 1024
        ),
    )(straggler, decode, *(pltpu.with_memory_space_constraint(v, pltpu.HBM) for v in (encode, patches, grad_embed, weight.T)))


def solution(mesh):
    return jax.shard_map(
        body,
        mesh=mesh,
        in_specs=(
            P(("dp", "fsdp"), None),
            P(("dp", "fsdp"), None),
            P(None, "fsdp"),
            P("dp"),
            P("dp"),
            P("dp", None),
        ),
        out_specs=(P(("dp", "fsdp"), None), P("dp", "fsdp")),
        check_vma=False,
    )
```

```python
import jax
import jax.numpy as jnp
from jax import lax
from jax.experimental import pallas as pl
from jax.experimental.pallas import tpu as pltpu
from jax.sharding import PartitionSpec as P

MESH = pl.DeviceIdType.MESH
F32 = jnp.float32
BF16 = jnp.bfloat16
RING = 8
X_LO = 4
P_SIZE = 384
DW = 3072
TOK = 256
SHARD = DW // 16
HALF = SHARD // 2
COLS = 2 * SHARD
PIECE = 96
PH = PIECE // 2
PLUS, MINUS = 0, 1
STEP = (1, -1)
SCALE = 8
I16 = jnp.int16


OWN_HOPS = (3, 4)
REACH = (1, 2, -1, -2, 3, 4, -3)


def scales(top):
    return jnp.floor(jnp.log2(jnp.maximum(top, 2.0 ** -100))) - 14.0


def code(v, over=0):
    e = scales(jnp.max(jnp.abs(v), axis=over, keepdims=True))
    return jnp.clip(jnp.round(v * jnp.exp2(-e)), -32767.0, 32767.0), e


def decoded(ref, rows):
    scale = jnp.exp2(ref[rows:rows + 1, :].astype(jnp.int32).astype(F32))
    return ref[0:rows, :].astype(jnp.int32).astype(F32) * scale


def kernel(strag, decode, enc_hbm, p_hbm, g_hbm, w_hbm, emb, out_ref,
           encode, g, p, gsib, psib, wt, t, q1, r1, s, s2, r2, u, s3, r3, msg, msgs,
           lsem, msem_s, msem_r, tsem_s, tsem_r, xsem_s, xsem_r, asem_s, asem_r, csem_s, csem_r, bsem_s, bsem_r,
           sem1_s, sem1_r, sem2_s, sem2_r, sem3_s, sem3_r):
    dp, fs = lax.axis_index("dp"), lax.axis_index("fsdp")
    core = lax.rem(dp, 2)
    xl = lax.rem(lax.div(dp, 2), X_LO)
    z = lax.div(dp, 2 * X_LO)
    xh = lax.div(fs, RING)
    y = lax.rem(fs, RING)
    x = xh * X_LO + xl

    def wrap(v):
        return lax.rem(v + RING, RING)

    def dev(x_, y_, z_, c_):
        return (z_ * 2 * X_LO + lax.rem(x_, X_LO) * 2 + c_, lax.div(x_, X_LO) * RING + y_)

    sib = (dp + 1 - 2 * core, fs)
    chip = lax.div(dp, 2)
    chips = 32
    following = lax.rem(chip + 1, chips)
    preceding = lax.rem(chip + chips - 1, chips)

    def remote(src, dst, ss, rs, to):
        return pltpu.make_async_remote_copy(src_ref=src, dst_ref=dst, send_sem=ss, recv_sem=rs,
                                            device_id=to, device_id_type=MESH)

    shard_rows = pl.ds(pl.multiple_of(fs * SHARD, SHARD), SHARD)
    def columns(h, c_):
        return pl.ds(pl.multiple_of(h * (DW // 2) + c_ * 2 * COLS, COLS), 2 * COLS)

    def load(src, dst, k):
        copy = pltpu.make_async_copy(src, dst, lsem.at[k])
        copy.start()
        return copy

    load_e = load(enc_hbm, encode, 0)
    load_w = load(w_hbm, wt.at[shard_rows], 1)
    load_p = load(p_hbm, p, 2)
    load_theirs = [load(g_hbm.at[:, columns(h, 1 - core)], g.at[:, columns(h, 1 - core)], 3 + h) for h in (0, 1)]
    load_mine = [load(g_hbm.at[:, columns(h, core)], g.at[:, columns(h, core)], 5 + h) for h in (0, 1)]

    barrier = pltpu.get_barrier_semaphore()
    partners = [sib]
    for k in (1, 2, RING - 2, RING - 1):
        partners.append(dev(lax.rem(x + k, RING), y, z, core))
        partners.append(dev(x, y, lax.rem(z + k, RING), core))
        partners.append(dev(x, lax.rem(y + k, RING), z, core))
    for other in (following, preceding):
        partners.append((2 * other, fs))
        partners.append((2 * other + 1, fs))
    for to in partners:
        pl.semaphore_signal(barrier, inc=1, device_id=to, device_id_type=MESH)

    load_e.wait()
    served = strag[0] * decode[0]
    row = lax.broadcasted_iota(jnp.int32, (8, 128), 0)
    msg[...] = jnp.where(row == 0, served * encode[0, 0], served * encode[0, 1])

    pl.semaphore_wait(barrier, len(partners))

    share_sib = remote(msg, msgs.at[0], msem_s.at[0], msem_r.at[0], sib)
    share_sib.start()
    share_next = [remote(msg, msgs.at[1], msem_s.at[1 + c], msem_r.at[1], (2 * following + c, fs)) for c in (0, 1)]

    @pl.when(core == 1)
    def _():
        for copy in share_next:
            copy.start()

    def unit(x_hi, y_, c_):
        return wt.at[pl.ds(pl.multiple_of((x_hi * RING + y_) * SHARD + c_ * HALF, 32), HALF)]

    def passed(block, k):
        return remote(block, block, bsem_s.at[k], bsem_r.at[k], sib)

    def own_at(way, hop, c_):
        return unit(xh, wrap(y - STEP[way] * hop), c_)

    def own_send(way, hop):
        block = own_at(way, hop, core)
        to = dev(x, wrap(y + STEP[way]), z, core)
        return remote(block, block, asem_s.at[way, hop], asem_r.at[way, hop], to)

    def own_pass(way, hop, c_):
        return passed(own_at(way, hop, c_), 4 * way + hop - 1)

    def own_hop(hop):
        for way in (PLUS, MINUS):
            if hop <= OWN_HOPS[way]:
                block = own_at(way, hop, core)
                remote(block, block, asem_s.at[way, hop - 1], asem_r.at[way, hop - 1], sib).wait_recv()
                if hop < OWN_HOPS[way]:
                    own_send(way, hop).start()
                own_pass(way, hop, core).start()

    def far_at(reach, c_):
        return unit(1 - xh, wrap(y - reach), c_)

    def far_send(k):
        reach = REACH[k]
        held = 0 if abs(reach) <= 2 else (2 if reach > 0 else -2)
        block = far_at(held, core)
        return remote(block, block, csem_s.at[k], csem_r.at[k], dev(x, wrap(y + reach - held), z, core))

    def far_pass(k, c_):
        return passed(far_at(REACH[k], c_), 8 + k)

    def far_arrive(k):
        block = far_at(REACH[k], core)
        remote(block, block, csem_s.at[k], csem_r.at[k], sib).wait_recv()

    load_w.wait()
    edge = (xl == 0) | (xl == X_LO - 1)
    outward = jnp.where(xl == 0, RING - 1, 1)
    own_unit = unit(xh, y, core)
    cross = [remote(own_unit, own_unit, xsem_s.at[k], xsem_r.at[0],
                    dev(lax.rem(x + (k + 1) * outward, RING), y, z, core)) for k in (0, 1)]

    @pl.when(edge)
    def _():
        for copy in cross:
            copy.start()

    for way in (PLUS, MINUS):
        own_send(way, 0).start()

    load_p.wait()
    tokens = [remote(p, psib, tsem_s.at[2], tsem_r.at[2], sib)]
    tokens[0].start()
    for h in (0, 1):
        load_theirs[h].wait()
        copy = remote(g.at[:, columns(h, 1 - core)], gsib.at[h], tsem_s.at[h], tsem_r.at[h], sib)
        copy.start()
        tokens.append(copy)
    for copy in load_mine:
        copy.wait()

    feature = lax.broadcasted_iota(jnp.int32, (P_SIZE, P_SIZE), 1)
    twelfth = jnp.right_shift(feature * 43691, 19)
    z_of = jnp.right_shift(feature * 10923, 19)
    place = (twelfth - X_LO * z_of) * PIECE + z_of * 12 + (feature - 12 * twelfth)
    out_row = lax.broadcasted_iota(jnp.int32, (P_SIZE, P_SIZE), 0)
    turn = (
        (out_row == feature).astype(F32).astype(BF16),
        (out_row == place).astype(F32).astype(BF16),
    )

    def features_first(q, tok):
        return lax.dot_general(turn[q], tok, (((1,), (1,)), ((), ())), preferred_element_type=F32).astype(BF16)

    for q in (0, 1):
        mine = features_first(q, p[...])
        for h in (0, 1):
            here = pl.ds(pl.multiple_of(h * (DW // 2) + core * 2 * COLS + q * COLS, COLS), COLS)
            term = jnp.dot(mine, g[:, here], preferred_element_type=F32)
            if q == 0:
                for k in range(RING):
                    t[0, k, h * PH:(h + 1) * PH, :] = term[k * PH:(k + 1) * PH]
            else:
                for k in range(X_LO):
                    t[1, h * X_LO + k, :, :] = term[k * PIECE:(k + 1) * PIECE]

    own_hop(1)
    crossed = far_at(0, core)
    remote(crossed, crossed, xsem_s.at[0], xsem_r.at[0], sib).wait_recv()
    for k in (1, 3, 0, 2):
        far_send(k).start()
    passed(crossed, 15).start()

    share_sib.wait_recv()
    remote(msg, msgs.at[1], msem_s.at[1], msem_r.at[1], sib).wait_recv()
    before = msgs[1, 1:2, 0:1]
    first_own, second_own = msg[0:1, 0:1], msg[1:2, 0:1]
    first_sib, second_sib = msgs[0, 0:1, 0:1], msgs[0, 1:2, 0:1]
    lower = core == 0
    scale_own = (first_own + jnp.where(lower, before, second_sib)).astype(F32) / (TOK * 16)
    scale_sib = (first_sib + jnp.where(lower, second_own, before)).astype(F32) / (TOK * 16)

    for copy in tokens:
        copy.wait_recv()

    pos = (z, x)

    def beside(q, v):
        return dev(x, y, v, core) if q == 0 else dev(v, y, z, core)

    turned = 1 - 2 * lax.rem(pos[0], 2), 1 - 2 * lax.rem(pos[1], 2)
    route = ((4, 2), (-3, -1), (3, 2), (-2, -1), (-1, -1), (2, 2), (1, 1))

    def along(q, k):
        slot = q1.at[q, k]
        return remote(slot, r1.at[q, k], sem1_s.at[q, k], sem1_r.at[q, k], beside(q, wrap(pos[q] + turned[q] * route[k][1])))

    def along_send(q, k):
        v = t[q, wrap(pos[q] + turned[q] * route[k][0])]
        for got in {5: (0, 1), 6: (2, 3)}.get(k, ()):
            along_wait(q, got)
            v += decoded(r1.at[q, got], PIECE)
        v, e = code(v)
        q1[q, k, 0:PIECE, :] = v.astype(jnp.int32).astype(I16)
        q1[q, k, PIECE:PIECE + SCALE, :] = jnp.broadcast_to(e, (SCALE, COLS)).astype(jnp.int32).astype(I16)
        along(q, k).start()

    def along_wait(q, k):
        slot = r1.at[q, k]
        remote(slot, slot, sem1_s.at[q, k], sem1_r.at[q, k], sib).wait_recv()

    for q in (0, 1):
        others = features_first(q, psib[...])
        for h in (0, 1):
            term = scale_sib * jnp.dot(others, gsib[h, :, q * COLS:(q + 1) * COLS], preferred_element_type=F32)
            if q == 0:
                for k in range(RING):
                    rows = slice(h * PH, (h + 1) * PH)
                    t[0, k, rows, :] = scale_own * t[0, k, rows, :] + term[k * PH:(k + 1) * PH]
            else:
                for k in range(X_LO):
                    at = h * X_LO + k
                    t[1, at, :, :] = scale_own * t[1, at, :, :] + term[k * PIECE:(k + 1) * PIECE]
        for k in range(5):
            along_send(q, k)

    own_hop(2)
    for k in (1, 3):
        far_arrive(k)
        for j in ((4, 5) if k == 1 else (6,)):
            far_send(j).start()
        far_pass(k, core).start()
    own_hop(3)
    for k in (5, 6):
        for q in (0, 1):
            along_send(q, k)
    own_hop(4)

    def embed_half(x_hi):
        def embed(j, carry):
            at = pl.multiple_of(x_hi * (DW // 2) + j * COLS, COLS)
            e = lax.dot_general(p[...], wt[pl.ds(at, COLS), :], (((1,), (1,)), ((), ())), preferred_element_type=F32)
            emb[:, pl.ds(at, COLS)] = e.astype(BF16)
            return carry

        lax.fori_loop(0, DW // 2 // COLS, embed, 0)

    for k in (0, 2, 4, 6, 5):
        far_arrive(k)
        far_pass(k, core).start()

    pos2 = (x, z)

    def across(q, j):
        k = wrap(pos2[q] + j - RING)
        return remote(s2.at[q, k], r2.at[q, j], sem2_s.at[q, j], sem2_r.at[q, j], beside(1 - q, k))

    for q in (0, 1):
        for k in (4, 5, 6):
            along_wait(q, k)
        total = t[q, pos[q]]
        for k in (4, 5, 6):
            total += decoded(r1.at[q, k], PIECE)
        s[q, 0:PIECE, :] = total
        s[q, PIECE:PIECE + 8, :] = jnp.zeros((8, COLS), F32)
    data_row = lax.broadcasted_iota(jnp.int32, (RING, 16, COLS), 1) < 12
    for q in (0, 1):
        v = jnp.stack([s[q, 12 * k:12 * k + 16, :] for k in range(RING)])
        v, e = code(jnp.where(data_row, v, 0.0), 1)
        s2[q] = jnp.where(data_row, v, e).astype(jnp.int32).astype(I16)
        for j in range(1, RING):
            across(q, j).start()

    for way in (PLUS, MINUS):
        for hop in range(1, OWN_HOPS[way] + 1):
            own_pass(way, hop, 1 - core).wait_recv()
    embed_half(xh)

    for k in range(7):
        far_pass(k, 1 - core).wait_recv()
    passed(far_at(0, 1 - core), 15).wait_recv()
    embed_half(1 - xh)

    def onward(q, par, c_):
        y_to = 4 * core + 2 * q + par
        return y_to, remote(s3.at[q, par, c_], r3.at[y], sem3_s.at[q, par, c_], sem3_r.at[y], dev(x, y_to, z, c_))

    for q in (0, 1):
        for j in range(1, RING):
            across(q, j).wait_recv()
        total = decoded(s2.at[q, pos2[q]], 12)
        for j in range(1, RING):
            total += decoded(r2.at[q, j], 12)
        u[q, 0:12, :] = total
        u[q, 12:16, :] = jnp.zeros((4, COLS), F32)
        for par in (0, 1):
            for c_ in (0, 1):
                s3[q, par, c_] = u[q, 6 * c_:6 * c_ + 8, par * SHARD:(par + 1) * SHARD]
                y_to, copy = onward(q, par, c_)
                self_ = (y_to == y) & (core == c_)

                @pl.when(self_)
                def _():
                    r3[y] = s3[q, par, c_]

                @pl.when(jnp.logical_not(self_))
                def _():
                    copy.start()

    summed_by = lax.div(y, 4)
    for k in range(RING):
        slot = r3.at[k]

        @pl.when(jnp.logical_not((y == k) & (core == summed_by)))
        def _():
            remote(slot, slot, sem3_s.at[0, 0, 0], sem3_r.at[k], sib).wait_recv()

    total = r3[0]
    for k in range(1, RING):
        total += r3[k]
    out_ref[...] = total[0:6]

    share_sib.wait_send()

    @pl.when(core == 1)
    def _():
        for copy in share_next:
            copy.wait_send()

    @pl.when(edge)
    def _():
        for copy in cross:
            copy.wait_send()

    for copy in tokens:
        copy.wait_send()
    passed(crossed, 15).wait_send()
    for way in (PLUS, MINUS):
        for hop in range(OWN_HOPS[way]):
            own_send(way, hop).wait_send()
            own_pass(way, hop + 1, core).wait_send()
    for k in range(7):
        far_send(k).wait_send()
        far_pass(k, core).wait_send()
        for q in (0, 1):
            along(q, k).wait_send()
    for q in (0, 1):
        for j in range(1, RING):
            across(q, j).wait_send()
        for par in (0, 1):
            for c_ in (0, 1):
                y_to, copy = onward(q, par, c_)

                @pl.when(jnp.logical_not((y_to == y) & (core == c_)))
                def _():
                    copy.wait_send()


def body(patches, grad_embed, weight, straggler, decode, encode):
    hbm = pl.BlockSpec(memory_space=pltpu.HBM)
    vmem = pl.BlockSpec(memory_space=pltpu.VMEM)
    smem = pl.BlockSpec(memory_space=pltpu.SMEM)
    dma = pltpu.SemaphoreType.DMA
    return pl.pallas_call(
        kernel,
        out_shape=(
            pltpu.VMEM((TOK, DW), BF16),
            pltpu.VMEM((6, SHARD), F32),
        ),
        in_specs=[smem] * 2 + [hbm] * 4,
        out_specs=(vmem, vmem),
        scratch_shapes=[
            pltpu.SMEM((1, 2), jnp.int32),
            pltpu.VMEM((TOK, DW), BF16),
            pltpu.VMEM((TOK, P_SIZE), BF16),
            pltpu.VMEM((2, TOK, 2 * COLS), BF16),
            pltpu.VMEM((TOK, P_SIZE), BF16),
            pltpu.VMEM((DW, P_SIZE), BF16),
            pltpu.VMEM((2, RING, PIECE, COLS), F32),
            pltpu.VMEM((2, 7, PIECE + SCALE, COLS), I16),
            pltpu.VMEM((2, 7, PIECE + SCALE, COLS), I16),
            pltpu.VMEM((2, PIECE + 8, COLS), F32),
            pltpu.VMEM((2, RING, 16, COLS), I16),
            pltpu.VMEM((2, RING, 16, COLS), I16),
            pltpu.VMEM((2, 16, COLS), F32),
            pltpu.VMEM((2, 2, 2, 8, SHARD), F32),
            pltpu.VMEM((RING, 8, SHARD), F32),
            pltpu.VMEM((8, 128), jnp.int32),
            pltpu.VMEM((2, 8, 128), jnp.int32),
            dma((7,)),
            dma((3,)), dma((2,)),
            dma((3,)), dma((3,)),
            dma((2,)), dma((1,)),
            dma((2, 4)), dma((2, 4)),
            dma((7,)), dma((7,)),
            dma((16,)), dma((16,)),
            dma((2, 7)), dma((2, 7)),
            dma((2, RING)), dma((2, RING)),
            dma((2, 2, 2)), dma((RING,)),
        ],
        compiler_params=pltpu.CompilerParams(
            collective_id=0, has_side_effects=True, vmem_limit_bytes=48 * 1024 * 1024
        ),
    )(straggler, decode, *(pltpu.with_memory_space_constraint(v, pltpu.HBM) for v in (encode, patches, grad_embed, weight.T)))


def solution(mesh):
    return jax.shard_map(
        body,
        mesh=mesh,
        in_specs=(
            P(("dp", "fsdp"), None),
            P(("dp", "fsdp"), None),
            P(None, "fsdp"),
            P("dp"),
            P("dp"),
            P("dp", None),
        ),
        out_specs=(P(("dp", "fsdp"), None), P("dp", "fsdp")),
        check_vma=False,
    )
```

```python
import jax
import jax.numpy as jnp
from jax import lax
from jax.experimental import pallas as pl
from jax.experimental.pallas import tpu as pltpu
from jax.sharding import PartitionSpec as P

MESH = pl.DeviceIdType.MESH
F32 = jnp.float32
BF16 = jnp.bfloat16
RING = 8
X_LO = 4
P_SIZE = 384
DW = 3072
TOK = 256
SHARD = DW // 16
HALF = SHARD // 2
COLS = 2 * SHARD
PIECE = 96
PH = PIECE // 2
PLUS, MINUS = 0, 1
STEP = (1, -1)
SCALE = 8
I16 = jnp.int16


OWN_HOPS = (3, 4)
REACH = (1, 2, -1, -2, 3, 4, -3)


def scales(top):
    return jnp.floor(jnp.log2(jnp.maximum(top, 2.0 ** -100))) - 14.0


def rounded(v, e):
    return jnp.clip(jnp.round(v * jnp.exp2(-e)), -32767.0, 32767.0)


def code(v, over=0):
    e = scales(jnp.max(jnp.abs(v), axis=over, keepdims=True))
    return rounded(v, e), e


def decoded(ref, rows):
    scale = jnp.exp2(ref[rows:rows + 1, :].astype(jnp.int32).astype(F32))
    return ref[0:rows, :].astype(jnp.int32).astype(F32) * scale


def kernel(strag, decode, enc_hbm, p_hbm, g_hbm, w_hbm, emb, out_ref,
           encode, g, p, gsib, psib, wt, t, ex, q1, r1, s, s2, r2, u, s3, r3, msg, msgs,
           lsem, msem_s, msem_r, tsem_s, tsem_r, xsem_s, xsem_r, asem_s, asem_r, csem_s, csem_r, bsem_s, bsem_r,
           sem1_s, sem1_r, sem2_s, sem2_r, sem3_s, sem3_r):
    dp, fs = lax.axis_index("dp"), lax.axis_index("fsdp")
    core = lax.rem(dp, 2)
    xl = lax.rem(lax.div(dp, 2), X_LO)
    z = lax.div(dp, 2 * X_LO)
    xh = lax.div(fs, RING)
    y = lax.rem(fs, RING)
    x = xh * X_LO + xl

    def wrap(v):
        return lax.rem(v + RING, RING)

    def dev(x_, y_, z_, c_):
        return (z_ * 2 * X_LO + lax.rem(x_, X_LO) * 2 + c_, lax.div(x_, X_LO) * RING + y_)

    sib = (dp + 1 - 2 * core, fs)
    chip = lax.div(dp, 2)
    chips = 32
    following = lax.rem(chip + 1, chips)
    preceding = lax.rem(chip + chips - 1, chips)

    def remote(src, dst, ss, rs, to):
        return pltpu.make_async_remote_copy(src_ref=src, dst_ref=dst, send_sem=ss, recv_sem=rs,
                                            device_id=to, device_id_type=MESH)

    shard_rows = pl.ds(pl.multiple_of(fs * SHARD, SHARD), SHARD)
    def columns(h, c_):
        return pl.ds(pl.multiple_of(h * (DW // 2) + c_ * 2 * COLS, COLS), 2 * COLS)

    def load(src, dst, k):
        copy = pltpu.make_async_copy(src, dst, lsem.at[k])
        copy.start()
        return copy

    load_e = load(enc_hbm, encode, 0)
    load_w = load(w_hbm, wt.at[shard_rows], 1)
    load_p = load(p_hbm, p, 2)
    load_theirs = [load(g_hbm.at[:, columns(h, 1 - core)], g.at[:, columns(h, 1 - core)], 3 + h) for h in (0, 1)]
    load_mine = [load(g_hbm.at[:, columns(h, core)], g.at[:, columns(h, core)], 5 + h) for h in (0, 1)]

    barrier = pltpu.get_barrier_semaphore()
    partners = [sib]
    for k in (1, 2, RING - 2, RING - 1):
        partners.append(dev(lax.rem(x + k, RING), y, z, core))
        partners.append(dev(x, y, lax.rem(z + k, RING), core))
        partners.append(dev(x, lax.rem(y + k, RING), z, core))
    for other in (following, preceding):
        partners.append((2 * other, fs))
        partners.append((2 * other + 1, fs))
    for to in partners:
        pl.semaphore_signal(barrier, inc=1, device_id=to, device_id_type=MESH)

    load_e.wait()
    served = strag[0] * decode[0]
    row = lax.broadcasted_iota(jnp.int32, (8, 128), 0)
    msg[...] = jnp.where(row == 0, served * encode[0, 0], served * encode[0, 1])

    pl.semaphore_wait(barrier, len(partners))

    share_sib = remote(msg, msgs.at[0], msem_s.at[0], msem_r.at[0], sib)
    share_sib.start()
    share_next = [remote(msg, msgs.at[1], msem_s.at[1 + c], msem_r.at[1], (2 * following + c, fs)) for c in (0, 1)]

    @pl.when(core == 1)
    def _():
        for copy in share_next:
            copy.start()

    def unit(x_hi, y_, c_):
        return wt.at[pl.ds(pl.multiple_of((x_hi * RING + y_) * SHARD + c_ * HALF, 32), HALF)]

    def passed(block, k):
        return remote(block, block, bsem_s.at[k], bsem_r.at[k], sib)

    def own_at(way, hop, c_):
        return unit(xh, wrap(y - STEP[way] * hop), c_)

    def own_send(way, hop):
        block = own_at(way, hop, core)
        to = dev(x, wrap(y + STEP[way]), z, core)
        return remote(block, block, asem_s.at[way, hop], asem_r.at[way, hop], to)

    def own_pass(way, hop, c_):
        return passed(own_at(way, hop, c_), 4 * way + hop - 1)

    def own_hop(hop):
        for way in (PLUS, MINUS):
            if hop <= OWN_HOPS[way]:
                block = own_at(way, hop, core)
                remote(block, block, asem_s.at[way, hop - 1], asem_r.at[way, hop - 1], sib).wait_recv()
                if hop < OWN_HOPS[way]:
                    own_send(way, hop).start()
                own_pass(way, hop, core).start()

    def far_at(reach, c_):
        return unit(1 - xh, wrap(y - reach), c_)

    def far_send(k):
        reach = REACH[k]
        held = 0 if abs(reach) <= 2 else (2 if reach > 0 else -2)
        block = far_at(held, core)
        return remote(block, block, csem_s.at[k], csem_r.at[k], dev(x, wrap(y + reach - held), z, core))

    def far_pass(k, c_):
        return passed(far_at(REACH[k], c_), 8 + k)

    def far_arrive(k):
        block = far_at(REACH[k], core)
        remote(block, block, csem_s.at[k], csem_r.at[k], sib).wait_recv()

    load_w.wait()
    edge = (xl == 0) | (xl == X_LO - 1)
    outward = jnp.where(xl == 0, RING - 1, 1)
    own_unit = unit(xh, y, core)
    cross = [remote(own_unit, own_unit, xsem_s.at[k], xsem_r.at[0],
                    dev(lax.rem(x + (k + 1) * outward, RING), y, z, core)) for k in (0, 1)]

    @pl.when(edge)
    def _():
        for copy in cross:
            copy.start()

    for way in (PLUS, MINUS):
        own_send(way, 0).start()

    load_p.wait()
    tokens = [remote(p, psib, tsem_s.at[2], tsem_r.at[2], sib)]
    tokens[0].start()
    for h in (0, 1):
        load_theirs[h].wait()
        copy = remote(g.at[:, columns(h, 1 - core)], gsib.at[h], tsem_s.at[h], tsem_r.at[h], sib)
        copy.start()
        tokens.append(copy)
    for copy in load_mine:
        copy.wait()

    feature = lax.broadcasted_iota(jnp.int32, (P_SIZE, P_SIZE), 1)
    twelfth = jnp.right_shift(feature * 43691, 19)
    z_of = jnp.right_shift(feature * 10923, 19)
    place = (twelfth - X_LO * z_of) * PIECE + z_of * 12 + (feature - 12 * twelfth)
    out_row = lax.broadcasted_iota(jnp.int32, (P_SIZE, P_SIZE), 0)
    turn = (
        (out_row == feature).astype(F32).astype(BF16),
        (out_row == place).astype(F32).astype(BF16),
    )

    def features_first(q, tok):
        return lax.dot_general(turn[q], tok, (((1,), (1,)), ((), ())), preferred_element_type=F32).astype(BF16)

    for q in (0, 1):
        mine = features_first(q, p[...])
        for h in (0, 1):
            here = pl.ds(pl.multiple_of(h * (DW // 2) + core * 2 * COLS + q * COLS, COLS), COLS)
            term = jnp.dot(mine, g[:, here], preferred_element_type=F32)
            if q == 0:
                for k in range(RING):
                    t[0, k, h * PH:(h + 1) * PH, :] = term[k * PH:(k + 1) * PH]
            else:
                for k in range(X_LO):
                    t[1, h * X_LO + k, :, :] = term[k * PIECE:(k + 1) * PIECE]

    own_hop(1)
    crossed = far_at(0, core)
    remote(crossed, crossed, xsem_s.at[0], xsem_r.at[0], sib).wait_recv()
    for k in (1, 3, 0, 2):
        far_send(k).start()
    passed(crossed, 15).start()

    share_sib.wait_recv()
    remote(msg, msgs.at[1], msem_s.at[1], msem_r.at[1], sib).wait_recv()
    before = msgs[1, 1:2, 0:1]
    first_own, second_own = msg[0:1, 0:1], msg[1:2, 0:1]
    first_sib, second_sib = msgs[0, 0:1, 0:1], msgs[0, 1:2, 0:1]
    lower = core == 0
    scale_own = (first_own + jnp.where(lower, before, second_sib)).astype(F32) / (TOK * 16)
    scale_sib = (first_sib + jnp.where(lower, second_own, before)).astype(F32) / (TOK * 16)

    for copy in tokens:
        copy.wait_recv()

    pos = (z, x)

    def beside(q, v):
        return dev(x, y, v, core) if q == 0 else dev(v, y, z, core)

    turned = 1 - 2 * lax.rem(pos[0], 2), 1 - 2 * lax.rem(pos[1], 2)
    route = ((4, 2), (-3, -1), (3, 2), (-2, -1), (-1, -1), (2, 2), (1, 1))

    def along(q, k):
        slot = q1.at[q, k]
        return remote(slot, r1.at[q, k], sem1_s.at[q, k], sem1_r.at[q, k], beside(q, wrap(pos[q] + turned[q] * route[k][1])))

    def along_send(q, k):
        piece = wrap(pos[q] + turned[q] * route[k][0])
        v = t[q, piece]
        for got in {5: (0, 1), 6: (2, 3)}.get(k, ()):
            along_wait(q, got)
            v += decoded(r1.at[q, got], PIECE)
        v, e = code(v) if k > 4 else (rounded(v, ex[q, piece, 0:1, :]), ex[q, piece, 0:1, :])
        q1[q, k, 0:PIECE, :] = v.astype(jnp.int32).astype(I16)
        q1[q, k, PIECE:PIECE + SCALE, :] = jnp.broadcast_to(e, (SCALE, COLS)).astype(jnp.int32).astype(I16)
        along(q, k).start()

    def along_wait(q, k):
        slot = r1.at[q, k]
        remote(slot, slot, sem1_s.at[q, k], sem1_r.at[q, k], sib).wait_recv()

    for q in (0, 1):
        others = features_first(q, psib[...])
        for h in (0, 1):
            term = scale_sib * jnp.dot(others, gsib[h, :, q * COLS:(q + 1) * COLS], preferred_element_type=F32)
            if q == 0:
                for k in range(RING):
                    rows = slice(h * PH, (h + 1) * PH)
                    t[0, k, rows, :] = scale_own * t[0, k, rows, :] + term[k * PH:(k + 1) * PH]
            else:
                for k in range(X_LO):
                    at = h * X_LO + k
                    t[1, at, :, :] = scale_own * t[1, at, :, :] + term[k * PIECE:(k + 1) * PIECE]
        tops = jnp.max(jnp.abs(t[q]), axis=1, keepdims=True)
        ex[q] = jnp.broadcast_to(scales(tops), (RING, SCALE, COLS))
        for k in range(5):
            along_send(q, k)

    own_hop(2)
    for k in (1, 3):
        far_arrive(k)
        for j in ((4, 5) if k == 1 else (6,)):
            far_send(j).start()
        far_pass(k, core).start()
    own_hop(3)
    for k in (5, 6):
        for q in (0, 1):
            along_send(q, k)
    own_hop(4)

    def embed_half(x_hi):
        def embed(j, carry):
            at = pl.multiple_of(x_hi * (DW // 2) + j * COLS, COLS)
            e = lax.dot_general(p[...], wt[pl.ds(at, COLS), :], (((1,), (1,)), ((), ())), preferred_element_type=F32)
            emb[:, pl.ds(at, COLS)] = e.astype(BF16)
            return carry

        lax.fori_loop(0, DW // 2 // COLS, embed, 0)

    for k in (0, 2, 4, 6, 5):
        far_arrive(k)
        far_pass(k, core).start()

    pos2 = (x, z)

    def across(q, j):
        k = wrap(pos2[q] + j - RING)
        return remote(s2.at[q, k], r2.at[q, j], sem2_s.at[q, j], sem2_r.at[q, j], beside(1 - q, k))

    for q in (0, 1):
        for k in (4, 5, 6):
            along_wait(q, k)
        total = t[q, pos[q]]
        for k in (4, 5, 6):
            total += decoded(r1.at[q, k], PIECE)
        s[q, 0:PIECE, :] = total
        s[q, PIECE:PIECE + 8, :] = jnp.zeros((8, COLS), F32)
    data_row = lax.broadcasted_iota(jnp.int32, (RING, 16, COLS), 1) < 12
    for q in (0, 1):
        v = jnp.stack([s[q, 12 * k:12 * k + 16, :] for k in range(RING)])
        v, e = code(jnp.where(data_row, v, 0.0), 1)
        s2[q] = jnp.where(data_row, v, e).astype(jnp.int32).astype(I16)
        for j in range(1, RING):
            across(q, j).start()

    for way in (PLUS, MINUS):
        for hop in range(1, OWN_HOPS[way] + 1):
            own_pass(way, hop, 1 - core).wait_recv()
    embed_half(xh)

    def onward(q, par, c_):
        y_to = 4 * core + 2 * q + par
        return y_to, remote(s3.at[q, par, c_], r3.at[y], sem3_s.at[q, par, c_], sem3_r.at[y], dev(x, y_to, z, c_))

    for q in (0, 1):
        for j in range(1, RING):
            across(q, j).wait_recv()
        total = decoded(s2.at[q, pos2[q]], 12)
        for j in range(1, RING):
            total += decoded(r2.at[q, j], 12)
        u[q, 0:12, :] = total
        u[q, 12:16, :] = jnp.zeros((4, COLS), F32)
        for par in (0, 1):
            for c_ in (0, 1):
                s3[q, par, c_] = u[q, 6 * c_:6 * c_ + 8, par * SHARD:(par + 1) * SHARD]
                y_to, copy = onward(q, par, c_)
                self_ = (y_to == y) & (core == c_)

                @pl.when(self_)
                def _():
                    r3[y] = s3[q, par, c_]

                @pl.when(jnp.logical_not(self_))
                def _():
                    copy.start()

    for k in range(7):
        far_pass(k, 1 - core).wait_recv()
    passed(far_at(0, 1 - core), 15).wait_recv()
    embed_half(1 - xh)

    summed_by = lax.div(y, 4)
    for k in range(RING):
        slot = r3.at[k]

        @pl.when(jnp.logical_not((y == k) & (core == summed_by)))
        def _():
            remote(slot, slot, sem3_s.at[0, 0, 0], sem3_r.at[k], sib).wait_recv()

    total = r3[0]
    for k in range(1, RING):
        total += r3[k]
    out_ref[...] = total[0:6]

    share_sib.wait_send()

    @pl.when(core == 1)
    def _():
        for copy in share_next:
            copy.wait_send()

    @pl.when(edge)
    def _():
        for copy in cross:
            copy.wait_send()

    for copy in tokens:
        copy.wait_send()
    passed(crossed, 15).wait_send()
    for way in (PLUS, MINUS):
        for hop in range(OWN_HOPS[way]):
            own_send(way, hop).wait_send()
            own_pass(way, hop + 1, core).wait_send()
    for k in range(7):
        far_send(k).wait_send()
        far_pass(k, core).wait_send()
        for q in (0, 1):
            along(q, k).wait_send()
    for q in (0, 1):
        for j in range(1, RING):
            across(q, j).wait_send()
        for par in (0, 1):
            for c_ in (0, 1):
                y_to, copy = onward(q, par, c_)

                @pl.when(jnp.logical_not((y_to == y) & (core == c_)))
                def _():
                    copy.wait_send()


def body(patches, grad_embed, weight, straggler, decode, encode):
    hbm = pl.BlockSpec(memory_space=pltpu.HBM)
    vmem = pl.BlockSpec(memory_space=pltpu.VMEM)
    smem = pl.BlockSpec(memory_space=pltpu.SMEM)
    dma = pltpu.SemaphoreType.DMA
    return pl.pallas_call(
        kernel,
        out_shape=(
            pltpu.VMEM((TOK, DW), BF16),
            pltpu.VMEM((6, SHARD), F32),
        ),
        in_specs=[smem] * 2 + [hbm] * 4,
        out_specs=(vmem, vmem),
        scratch_shapes=[
            pltpu.SMEM((1, 2), jnp.int32),
            pltpu.VMEM((TOK, DW), BF16),
            pltpu.VMEM((TOK, P_SIZE), BF16),
            pltpu.VMEM((2, TOK, 2 * COLS), BF16),
            pltpu.VMEM((TOK, P_SIZE), BF16),
            pltpu.VMEM((DW, P_SIZE), BF16),
            pltpu.VMEM((2, RING, PIECE, COLS), F32),
            pltpu.VMEM((2, RING, SCALE, COLS), F32),
            pltpu.VMEM((2, 7, PIECE + SCALE, COLS), I16),
            pltpu.VMEM((2, 7, PIECE + SCALE, COLS), I16),
            pltpu.VMEM((2, PIECE + 8, COLS), F32),
            pltpu.VMEM((2, RING, 16, COLS), I16),
            pltpu.VMEM((2, RING, 16, COLS), I16),
            pltpu.VMEM((2, 16, COLS), F32),
            pltpu.VMEM((2, 2, 2, 8, SHARD), F32),
            pltpu.VMEM((RING, 8, SHARD), F32),
            pltpu.VMEM((8, 128), jnp.int32),
            pltpu.VMEM((2, 8, 128), jnp.int32),
            dma((7,)),
            dma((3,)), dma((2,)),
            dma((3,)), dma((3,)),
            dma((2,)), dma((1,)),
            dma((2, 4)), dma((2, 4)),
            dma((7,)), dma((7,)),
            dma((16,)), dma((16,)),
            dma((2, 7)), dma((2, 7)),
            dma((2, RING)), dma((2, RING)),
            dma((2, 2, 2)), dma((RING,)),
        ],
        compiler_params=pltpu.CompilerParams(
            collective_id=0, has_side_effects=True, vmem_limit_bytes=48 * 1024 * 1024
        ),
    )(straggler, decode, *(pltpu.with_memory_space_constraint(v, pltpu.HBM) for v in (encode, patches, grad_embed, weight.T)))


def solution(mesh):
    return jax.shard_map(
        body,
        mesh=mesh,
        in_specs=(
            P(("dp", "fsdp"), None),
            P(("dp", "fsdp"), None),
            P(None, "fsdp"),
            P("dp"),
            P("dp"),
            P("dp", None),
        ),
        out_specs=(P(("dp", "fsdp"), None), P("dp", "fsdp")),
        check_vma=False,
    )
```
